256 devices in a mesh: row: 8 (over x, y_lo), col: 32 (over y_hi, z, core).
Axes of the slice: x: 4, y: 4 (y_hi: 2, y_lo: 2; y = y_hi * 2 + y_lo), z: 8, core: 2. Of those that a mesh axis runs over, the one named last changes fastest.
Arguments:
- saved_inverse: float32 [4, 8, 512, 1, 32, 512], P(None, 'row', None, None, 'col'), may hold values from -0.046875 to 0.046875
- inverse_adjoint: float32 [4, 8, 512, 1, 32, 512], P(None, 'row', None, None, 'col'), may hold values from -6 to 6
Outputs:
- panel_adjoint: float32 [1024, 1, 32, 512], P('row', None, 'col')
The draws below stay inside these ranges and needn't reach their ends.
All inputs are finite; a program needn't handle non-finite values.
Results may differ from the reference program's by a relative error of at most 0.000084.
Values sent between devices are 32-bit elements; how exact they have to be, the bound alone decides.
No kernel may reach another device: no remote copies, remote signals or barrier semaphores. Data moves between devices by JAX's collectives and lax.ppermute only.
A program may use at most 128 MiB of HBM per device.

```python
import jax
import jax.numpy as jnp
from jax import lax

M = 16384
NB = 512
K = 1024
START = 8192
CR = 4
CC = 1
N_ROW = 8
N_COL = 32


def block_levels(rng, shape, pieces, least, high):
    level, own = 1.0, jax.random.fold_in(rng, 6)
    for dim, shards_of in pieces:
        steps = jnp.exp(jax.random.uniform(jax.random.fold_in(own, dim), (shards_of,), jnp.float32, least / len(pieces), high / len(pieces)))
        level = level * jnp.repeat(steps, shape[dim] // shards_of).reshape([-1 if axis == dim else 1 for axis in range(len(shape))])
    return level


def scatter_about(rng, shape, scale, limit, pieces=(), held_as=jnp.bfloat16):
    entries = jax.random.normal(rng, shape, jnp.float32) * scale
    if len(pieces) > 0:
        entries = block_levels(rng, shape, pieces, -0.22, 0.18) * entries
    return jnp.clip(entries, min=-limit, max=limit).astype(held_as)


def setup_inputs(seed: int = 0) -> dict:
    arg_keys = jax.random.split(jax.random.key(seed), 3)
    saved_inverse = scatter_about(arg_keys[0], (CR, N_ROW, NB, CC, N_COL, NB), M ** -0.5, 0.046875, ((1, 8), (4, 32)), jnp.float32)
    inverse_adjoint = scatter_about(arg_keys[1], (CR, N_ROW, NB, CC, N_COL, NB), 1.0, 6.0, ((1, 8), (4, 32)), jnp.float32)
    return {"saved_inverse": saved_inverse, "inverse_adjoint": inverse_adjoint}


def reference(saved_inverse, inverse_adjoint):
    inverse = saved_inverse.reshape(M, M)
    positions = jnp.arange(M, dtype=jnp.int32)
    lower = jnp.where(positions[None, :] <= positions[:, None], inverse, 0.0)
    panel_data = lower[START:START + K]
    adjoint = inverse_adjoint.reshape(M, M)
    products = jnp.dot(adjoint, panel_data.T, precision=lax.Precision.HIGHEST, preferred_element_type=jnp.float32)
    result = -jnp.dot(products.T, lower, precision=lax.Precision.HIGHEST, preferred_element_type=jnp.float32)
    panel_col = jnp.arange(K, dtype=jnp.int32)
    result = jnp.where(positions[None, :] >= START + panel_col[:, None], result, 0.0)
    return result.reshape(K, CC, N_COL, NB)
```

```python
import jax
import jax.numpy as jnp
from jax import lax
from jax.sharding import Mesh, PartitionSpec as P

M = 16384
K = 1024
TILE = 512
START_TILE = 16
ROWS = ("x", "yl")
COLS = ("yh", "z", "core")


def ring(n, step):
    return [(i, (i + step) % n) for i in range(n)]


def pick(blocks, i):
    return lax.dynamic_index_in_dim(blocks, lax.rem(i + 2 * blocks.shape[0], blocks.shape[0]), 0, keepdims=False)


def spread_along_x(tile):
    x = lax.axis_index("x")
    half = TILE // 2
    top, bottom = tile[:half], tile[half:]
    swap = ring(2, 1)
    right1 = lax.ppermute(top, "x", [(0, 1)])
    left1 = lax.ppermute(bottom, "x", [(0, 3)])
    first = jnp.where(x == 3, left1, jnp.where(x == 1, right1, top))
    other1 = lax.ppermute(first, "yl", swap)
    right2 = lax.ppermute(jnp.where(x == 0, bottom, right1), "x", [(0, 1), (1, 2)])
    left2 = lax.ppermute(jnp.where(x == 0, top, left1), "x", [(0, 3), (3, 2)])
    own_top = jnp.where(x == 0, top, jnp.where(x == 1, right1, jnp.where(x == 2, right2, left2)))
    own_bottom = jnp.where(x == 0, bottom, jnp.where(x == 1, right2, jnp.where(x == 2, left2, left1)))
    quarter = half // 2
    both = jnp.concatenate([own_top[quarter:], own_bottom[quarter:]], 0)
    second = jnp.where(x == 2, both, jnp.where(x == 3, own_top, own_bottom))
    other2 = lax.ppermute(second, "yl", swap)
    right3 = lax.ppermute(other1[:quarter], "x", [(1, 2)])
    left3 = lax.ppermute(other1[:quarter], "x", [(3, 2)])
    other_top = jnp.where(
        x == 2, jnp.concatenate([right3, other2[:quarter]], 0), jnp.where(x == 3, other2, other1)
    )
    other_bottom = jnp.where(
        x == 2, jnp.concatenate([left3, other2[quarter:]], 0), jnp.where(x == 3, other1, other2)
    )
    return jnp.concatenate([own_top, own_bottom], 0), jnp.concatenate([other_top, other_bottom], 0)


def reduce_scatter_z(blocks):
    z = lax.axis_index("z")
    left = pick(blocks, z - 4)
    left = lax.ppermute(left, "z", ring(8, -1)) + pick(blocks, z - 3)
    right = pick(blocks, z + 3)
    for s in (2, 1):
        left = lax.ppermute(left, "z", ring(8, -1)) + pick(blocks, z - s)
        right = lax.ppermute(right, "z", ring(8, 1)) + pick(blocks, z + s)
    return lax.ppermute(left, "z", ring(8, -1)) + lax.ppermute(right, "z", ring(8, 1)) + pick(blocks, z)


def all_gather_z(block):
    held = {0: block}
    up, down = block, block
    for s in range(1, 5):
        up = lax.ppermute(up, "z", ring(8, -1))
        held[s] = up
        if s < 4:
            down = lax.ppermute(down, "z", ring(8, 1))
            held[8 - s] = down
    return jnp.concatenate([held[s] for s in range(8)], 0)


def dot(a, b, dims):
    return lax.dot_general(
        a, b, (dims, ((), ())), precision=lax.Precision.HIGH, preferred_element_type=jnp.float32
    )


def per_device(saved_inverse, inverse_adjoint):
    x, yl, yh, z, core = (lax.axis_index(n) for n in ("x", "yl", "yh", "z", "core"))
    row_at = 2 * x + yl
    col_at = 16 * yh + 2 * z + core
    pos = jnp.arange(TILE, dtype=jnp.int32)
    col_global = col_at * TILE + pos
    core_swap = ring(2, 1)

    w = saved_inverse[2:4].reshape(2, TILE, TILE)
    adj = inverse_adjoint[2:4].reshape(2, TILE, TILE)
    adj_mine = pick(adj, core)
    adj_partner = lax.ppermute(pick(adj, core + 1), "core", core_swap)

    own, other = spread_along_x(w[0])

    def masked(tile, row_tile):
        return jnp.where(col_global[None, :] <= (row_tile * TILE + pos)[:, None], tile, 0.0)

    panels = (masked(own, START_TILE + yl), masked(other, START_TILE + 1 - yl))
    w_mine = masked(pick(w, core), START_TILE + row_at + 8 * core)
    w_partner = masked(pick(w, core + 1), START_TILE + row_at + 8 * (1 - core))
    results = []
    for panel in panels:
        partner_panel = lax.ppermute(panel, "core", core_swap)
        part = dot(panel, adj_mine, ((1,), (1,))) + dot(partner_panel, adj_partner, ((1,), (1,)))
        summed = reduce_scatter_z(part.reshape(8, TILE // 8, TILE))
        summed = summed + lax.ppermute(summed, "yh", [(0, 1)])
        mine = all_gather_z(summed)
        partner = lax.ppermute(mine, "core", core_swap)
        results.append(dot(mine, w_mine, ((1,), (0,))) + dot(partner, w_partner, ((1,), (0,))))
    result = jnp.stack(results, 0).reshape(2 * 8, TILE // 8, TILE)

    def block_for(row):
        tile = row // 4
        at = 8 * lax.rem(tile + yl, 2)
        b = 2 * lax.rem(row, 4) + 16 - z
        return jnp.concatenate([pick(result, at + lax.rem(b, 8)), pick(result, at + lax.rem(b + 1, 8))], 0)

    total = block_for(row_at)
    for dx in (2, 1, 3, 0):
        for dy in (1, 0):
            if dx or dy:
                to = 2 * lax.rem(x + dx, 4) + lax.rem(yl + dy, 2)
                pairs = [
                    (2 * i + j, 2 * ((i + dx) % 4) + (j + dy) % 2) for i in range(4) for j in range(2)
                ]
                total = total + lax.ppermute(block_for(to), ROWS, pairs)
    kept = K // 8
    panel_col = row_at * kept + jnp.arange(kept, dtype=jnp.int32)
    out = jnp.where(col_global[None, :] >= M // 2 + panel_col[:, None], -total, 0.0)
    return out.reshape(kept, 1, 1, TILE)


def solution(mesh):
    fine = Mesh(mesh.devices.reshape(4, 2, 2, 8, 2), ROWS + COLS)
    placed = P(None, ROWS, None, None, COLS, None)
    return jax.shard_map(
        per_device,
        mesh=fine,
        in_specs=(placed, placed),
        out_specs=P(ROWS, None, COLS, None),
        check_vma=False,
    )
```

```python
import jax
import jax.numpy as jnp
from jax import lax
from jax.sharding import Mesh, PartitionSpec as P


M = 16384
K = 1024
TILE = 512
START_TILE = 16
ROWS = ("x", "yl")
COLS = ("yh", "z", "core")


def ring(n, step):
    return [(i, (i + step) % n) for i in range(n)]


def pick(blocks, i):
    return lax.dynamic_index_in_dim(blocks, lax.rem(i + 2 * blocks.shape[0], blocks.shape[0]), 0, keepdims=False)


def spread_along_x(tile):
    x = lax.axis_index("x")
    half = TILE // 2
    top, bottom = tile[:half], tile[half:]
    swap = ring(2, 1)
    right1 = lax.ppermute(top, "x", [(0, 1)])
    left1 = lax.ppermute(bottom, "x", [(0, 3)])
    first, to_right, to_left = lax.optimization_barrier(
        (
            jnp.where(x == 3, left1, jnp.where(x == 1, right1, top)),
            jnp.where(x == 0, bottom, right1),
            jnp.where(x == 0, top, left1),
        )
    )
    other1 = lax.ppermute(first, "yl", swap)
    right2 = lax.ppermute(to_right, "x", [(0, 1), (1, 2)])
    left2 = lax.ppermute(to_left, "x", [(0, 3), (3, 2)])
    own_top = jnp.where(x == 0, top, jnp.where(x == 1, right1, jnp.where(x == 2, right2, left2)))
    own_bottom = jnp.where(x == 0, bottom, jnp.where(x == 1, right2, jnp.where(x == 2, left2, left1)))
    quarter = half // 2
    both = jnp.concatenate([own_top[quarter:], own_bottom[quarter:]], 0)
    second = jnp.where(x == 2, both, jnp.where(x == 3, own_top, own_bottom))
    other2 = lax.ppermute(second, "yl", swap)
    right3 = lax.ppermute(other1[:quarter], "x", [(1, 2)])
    left3 = lax.ppermute(other1[:quarter], "x", [(3, 2)])
    other_top = jnp.where(
        x == 2, jnp.concatenate([right3, other2[:quarter]], 0), jnp.where(x == 3, other2, other1)
    )
    other_bottom = jnp.where(
        x == 2, jnp.concatenate([left3, other2[quarter:]], 0), jnp.where(x == 3, other1, other2)
    )
    return jnp.concatenate([own_top, own_bottom], 0), jnp.concatenate([other_top, other_bottom], 0)


def reduce_scatter_z(blocks):
    z = lax.axis_index("z")
    left = pick(blocks, z - 4)
    left = lax.ppermute(left, "z", ring(8, -1)) + pick(blocks, z - 3)
    right = pick(blocks, z + 3)
    for s in (2, 1):
        left = lax.ppermute(left, "z", ring(8, -1)) + pick(blocks, z - s)
        right = lax.ppermute(right, "z", ring(8, 1)) + pick(blocks, z + s)
    return lax.ppermute(left, "z", ring(8, -1)) + lax.ppermute(right, "z", ring(8, 1)) + pick(blocks, z)


def all_gather_z(block):
    held = {0: block}
    up, down = block, block
    for s in range(1, 5):
        up = lax.ppermute(up, "z", ring(8, -1))
        held[s] = up
        if s < 4:
            down = lax.ppermute(down, "z", ring(8, 1))
            held[8 - s] = down
    return jnp.concatenate([held[s] for s in range(8)], 0)


def dot(a, b, dims):
    return lax.dot_general(
        a, b, (dims, ((), ())), precision=lax.Precision.HIGH, preferred_element_type=jnp.float32
    )


def panel_adjoint(saved_inverse, inverse_adjoint):
    x, yl, yh, z, core = (lax.axis_index(n) for n in ("x", "yl", "yh", "z", "core"))
    row_at = 2 * x + yl
    col_at = 16 * yh + 2 * z + core
    pos = jnp.arange(TILE, dtype=jnp.int32)
    col_global = col_at * TILE + pos
    core_swap = ring(2, 1)

    w = saved_inverse[2:4].reshape(2, TILE, TILE)
    adj = inverse_adjoint[2:4].reshape(2, TILE, TILE)
    adj_mine = pick(adj, core)
    adj_partner = lax.ppermute(pick(adj, core + 1), "core", core_swap)

    own, other = spread_along_x(w[0])

    def masked(tile, row_tile):
        return jnp.where(col_global[None, :] <= (row_tile * TILE + pos)[:, None], tile, 0.0)

    own, w_mine, w_partner = lax.optimization_barrier(
        (
            masked(own, START_TILE + yl),
            masked(pick(w, core), START_TILE + row_at + 8 * core),
            masked(pick(w, core + 1), START_TILE + row_at + 8 * (1 - core)),
        )
    )
    gathered = []
    for panel in (own, masked(other, START_TILE + 1 - yl)):
        partner_panel = lax.ppermute(panel, "core", core_swap)
        part = dot(panel, adj_mine, ((1,), (1,))) + dot(partner_panel, adj_partner, ((1,), (1,)))
        summed = reduce_scatter_z(part.reshape(8, TILE // 8, TILE))
        summed = summed + lax.ppermute(summed, "yh", [(0, 1)])
        mine = all_gather_z(summed)
        partner = lax.ppermute(mine, "core", core_swap)
        gathered.append(dot(mine, w_mine, ((1,), (0,))) + dot(partner, w_partner, ((1,), (0,))))
    result = jnp.concatenate(gathered, 0).reshape(2 * 8, TILE // 8, TILE)

    def block_for(row):
        tile = row // 4
        at = 8 * lax.rem(tile + yl, 2)
        b = 2 * lax.rem(row, 4) + 16 - z
        return jnp.concatenate([pick(result, at + lax.rem(b, 8)), pick(result, at + lax.rem(b + 1, 8))], 0)

    total = block_for(row_at)
    for dx in (2, 1, 3, 0):
        for dy in (1, 0):
            if dx or dy:
                to = 2 * lax.rem(x + dx, 4) + lax.rem(yl + dy, 2)
                pairs = [
                    (2 * i + j, 2 * ((i + dx) % 4) + (j + dy) % 2) for i in range(4) for j in range(2)
                ]
                total = total + lax.ppermute(block_for(to), ROWS, pairs)
    kept = K // 8
    panel_col = row_at * kept + jnp.arange(kept, dtype=jnp.int32)
    out = jnp.where(col_global[None, :] >= M // 2 + panel_col[:, None], -total, 0.0)
    return out.reshape(kept, 1, 1, TILE)


def solution(mesh):
    fine = Mesh(mesh.devices.reshape(4, 2, 2, 8, 2), ROWS + COLS)
    placed = P(None, ROWS, None, None, COLS, None)
    return jax.shard_map(
        panel_adjoint,
        mesh=fine,
        in_specs=(placed, placed),
        out_specs=P(ROWS, None, COLS, None),
        check_vma=False,
    )
```

```python
import jax
import jax.numpy as jnp
from jax import lax
from jax.sharding import Mesh, PartitionSpec as P


M = 16384
K = 1024
TILE = 512
START_TILE = 16
ROWS = ("x", "yl")
COLS = ("yh", "z", "core")


def ring(n, step):
    return [(i, (i + step) % n) for i in range(n)]


def pick(blocks, i):
    return lax.dynamic_index_in_dim(blocks, lax.rem(i + 2 * blocks.shape[0], blocks.shape[0]), 0, keepdims=False)


def spread_along_x(tile):
    x = lax.axis_index("x")
    half = TILE // 2
    top, bottom = tile[:half], tile[half:]
    swap = ring(2, 1)
    right1 = lax.ppermute(top, "x", [(0, 1)])
    left1 = lax.ppermute(bottom, "x", [(0, 3)])
    first, to_right, to_left = lax.optimization_barrier(
        (
            jnp.where(x == 3, left1, jnp.where(x == 1, right1, top)),
            jnp.where(x == 0, bottom, right1),
            jnp.where(x == 0, top, left1),
        )
    )
    other1 = lax.ppermute(first, "yl", swap)
    right2 = lax.ppermute(to_right, "x", [(0, 1), (1, 2)])
    left2 = lax.ppermute(to_left, "x", [(0, 3), (3, 2)])
    own_top = jnp.where(x == 0, top, jnp.where(x == 1, right1, jnp.where(x == 2, right2, left2)))
    own_bottom = jnp.where(x == 0, bottom, jnp.where(x == 1, right2, jnp.where(x == 2, left2, left1)))
    quarter = half // 2
    both = jnp.concatenate([own_top[quarter:], own_bottom[quarter:]], 0)
    second = jnp.where(x == 2, both, jnp.where(x == 3, own_top, own_bottom))
    other2 = lax.ppermute(second, "yl", swap)
    right3 = lax.ppermute(other1[:quarter], "x", [(1, 2)])
    left3 = lax.ppermute(other1[:quarter], "x", [(3, 2)])
    other_top = jnp.where(
        x == 2, jnp.concatenate([right3, other2[:quarter]], 0), jnp.where(x == 3, other2, other1)
    )
    other_bottom = jnp.where(
        x == 2, jnp.concatenate([left3, other2[quarter:]], 0), jnp.where(x == 3, other1, other2)
    )
    return jnp.concatenate([own_top, own_bottom], 0), jnp.concatenate([other_top, other_bottom], 0)


def reduce_scatter_z(blocks):
    z = lax.axis_index("z")
    left = pick(blocks, z - 4)
    left = lax.ppermute(left, "z", ring(8, -1)) + pick(blocks, z - 3)
    right = pick(blocks, z + 3)
    for s in (2, 1):
        left = lax.ppermute(left, "z", ring(8, -1)) + pick(blocks, z - s)
        right = lax.ppermute(right, "z", ring(8, 1)) + pick(blocks, z + s)
    return lax.ppermute(left, "z", ring(8, -1)) + lax.ppermute(right, "z", ring(8, 1)) + pick(blocks, z)


def all_gather_z(block):
    held = {0: block}
    up, down = block, block
    for s in range(1, 5):
        up = lax.ppermute(up, "z", ring(8, -1))
        held[s] = up
        if s < 4:
            down = lax.ppermute(down, "z", ring(8, 1))
            held[8 - s] = down
    return jnp.concatenate([held[s] for s in range(8)], 0)


def dot(a, b, dims):
    return lax.dot_general(
        a, b, (dims, ((), ())), precision=lax.Precision.HIGH, preferred_element_type=jnp.float32
    )


def panel_adjoint(saved_inverse, inverse_adjoint):
    x, yl, yh, z, core = (lax.axis_index(n) for n in ("x", "yl", "yh", "z", "core"))
    row_at = 2 * x + yl
    col_at = 16 * yh + 2 * z + core
    pos = jnp.arange(TILE, dtype=jnp.int32)
    col_global = col_at * TILE + pos
    core_swap = ring(2, 1)

    w = saved_inverse[2:4].reshape(2, TILE, TILE)
    adj = inverse_adjoint[2:4].reshape(2, TILE, TILE)
    adj_mine = pick(adj, core)
    adj_partner = lax.ppermute(pick(adj, core + 1), "core", core_swap)

    own, other = spread_along_x(w[0])

    def masked(tile, row_tile):
        return jnp.where(col_global[None, :] <= (row_tile * TILE + pos)[:, None], tile, 0.0)

    own, w_mine, w_partner = lax.optimization_barrier(
        (
            masked(own, START_TILE + yl),
            masked(pick(w, core), START_TILE + row_at + 8 * core),
            masked(pick(w, core + 1), START_TILE + row_at + 8 * (1 - core)),
        )
    )
    gathered = []
    for panel in (own, masked(other, START_TILE + 1 - yl)):
        partner_panel = lax.ppermute(panel, "core", core_swap)
        part = dot(panel, adj_mine, ((1,), (1,))) + dot(partner_panel, adj_partner, ((1,), (1,)))
        summed = reduce_scatter_z(part.reshape(8, TILE // 8, TILE))
        summed = summed + lax.ppermute(summed, "yh", [(0, 1)])
        mine = all_gather_z(summed)
        partner = lax.ppermute(mine, "core", core_swap)
        gathered.append(dot(mine, w_mine, ((1,), (0,))) + dot(partner, w_partner, ((1,), (0,))))
    result = jnp.concatenate(gathered, 0).reshape(2 * 8, TILE // 8, TILE)

    def block_for(row):
        tile = row // 4
        at = 8 * lax.rem(tile + yl, 2)
        b = 2 * lax.rem(row, 4) + 16 - z
        return jnp.concatenate([pick(result, at + lax.rem(b, 8)), pick(result, at + lax.rem(b + 1, 8))], 0)

    total = block_for(row_at)
    for dx, dy in ((1, 1), (3, 1), (2, 0), (0, 1), (2, 1), (1, 0), (3, 0)):
        to = 2 * lax.rem(x + dx, 4) + lax.rem(yl + dy, 2)
        pairs = [(2 * i + j, 2 * ((i + dx) % 4) + (j + dy) % 2) for i in range(4) for j in range(2)]
        total = total + lax.ppermute(block_for(to), ROWS, pairs)
    kept = K // 8
    panel_col = row_at * kept + jnp.arange(kept, dtype=jnp.int32)
    out = jnp.where(col_global[None, :] >= M // 2 + panel_col[:, None], -total, 0.0)
    return out.reshape(kept, 1, 1, TILE)


def solution(mesh):
    fine = Mesh(mesh.devices.reshape(4, 2, 2, 8, 2), ROWS + COLS)
    placed = P(None, ROWS, None, None, COLS, None)
    return jax.shard_map(
        panel_adjoint,
        mesh=fine,
        in_specs=(placed, placed),
        out_specs=P(ROWS, None, COLS, None),
        check_vma=False,
    )
```
